32 devices in a mesh: groups: 2 (over x), tok: 16 (over z, y, core).
Axes of the slice: x: 2, y: 2, z: 4, core: 2. Of those that a mesh axis runs over, the one named last changes fastest.
Arguments:
- vis_query: bfloat16 [8192, 1280], P(('groups', 'tok')), parts along dimension 0, may hold values from -180 to 180
- vis_keyvalue: bfloat16 [2, 8192, 1280], P(None, ('groups', 'tok')), parts along dimension 1, may hold values from -6 to 6
- vis_residual: bfloat16 [8192, 1280], P(('groups', 'tok')), parts along dimension 0, may hold values from -4 to 4
- vis_out_weight: bfloat16 [1280, 1280], P('tok'), may hold values from -0.15625 to 0.15625
- vis_out_bias: float32 [1280], replicated, may hold values from -4 to 4
- image_units: int32 [96], P('groups'), parts along dimension 0, may hold values from 1 to 32, 1024 in all
- text_embed: bfloat16 [8192, 5120], P(('groups', 'tok')), parts along dimension 0, may hold values from -6 to 6
- lm_gain: float32 [5120], replicated, may hold values from 0.1 to 1.9
- lm_kv_weight: bfloat16 [5120, 2048], P(None, 'tok'), may hold values from -0.078125 to 0.078125
- lm_kv_bias: float32 [2048], replicated, may hold values from -6 to 6
- text_positions: int32 [8192], P(('groups', 'tok')), parts along dimension 0, may hold values from 0 to 4095
- image_destination: int32 [2048, 1], P(('groups', 'tok')), parts along dimension 0, may hold values from 0 to 15; in each aligned block of 64 rows (0 to 63, 64 to 127, ...) at most 8 rows name the same one
- image_positions: int32 [3, 4096], P(None, ('groups', 'tok')), parts along dimension 1, may hold values from 0 to 4095
Outputs:
- text_cache: bfloat16 [8192, 2048], P(('groups', 'tok')), parts along dimension 0
- image_cache: bfloat16 [4096, 2048], P(('groups', 'tok')), parts along dimension 0
The draws below stay inside these ranges and needn't reach their ends.
There are 2 independent parts, one for each index of `groups`. The reference program is written for one: setup_inputs(seed, part) draws one part's arguments, and reference() takes and returns one part's arrays. A program takes and returns all parts, laid end to end along the dimension named above; an argument that names none is the same for every part. Nothing has to cross between parts.
Inputs may be any that keep to these rules, and one draw needn't show every extreme that they name: `image_units`: each image spans whole merged rows; entries sum to 1024 and one reaches the largest value. `image_destination`: among the 64 rows of one device no destination appears more than 8 times, and some device's rows reach that count.
All inputs are finite; a program needn't handle non-finite values.
Results may differ from the reference program's by a relative error of at most 0.0052.
Values may be sent and summed in bfloat16 or wider, within the bound.
No kernel may reach another device: no remote copies, remote signals or barrier semaphores. Data moves between devices by JAX's collectives and lax.ppermute only.
A program may use at most 128 MiB of HBM per device.

```python
import math
import jax
import jax.numpy as jnp
import numpy as np
from jax import lax

VIS_WIDTH = 1280
VIS_HEADS = 16
KV_HEADS = 8
LM_HEAD = 128
LM_WIDTH = 5120
KV_WIDTH = 2048
PATCH_DEV = 256
POS_LIMIT = 4096
UNITS_DEV = 64
CAP = 8
SLOTS_DEV = 128
PATCHES = 4096
UNITS = 1024
TEXT = 4096
IMG_SLOTS = 2048
IMAGES = 48
DESTS = 16
N_TOK = 16


def draw_keys(key):
    keys = jnp.clip(jax.random.normal(jax.random.fold_in(key, 7001), (PATCHES, VIS_WIDTH), jnp.float32), -6.0, 6.0)
    return keys


def draw_vis_keyvalue(key, part):
    keys = draw_keys(key)
    values = jnp.clip(jax.random.normal(jax.random.fold_in(key, 7004), (PATCHES, VIS_WIDTH), jnp.float32), -6.0, 6.0)
    return jnp.stack([keys, values]).astype(jnp.bfloat16)


def draw_vis_query(key, part):
    fresh = jnp.clip(jax.random.normal(jax.random.fold_in(key, 7002), (PATCHES, VIS_WIDTH), jnp.float32), -6.0, 6.0)
    return fresh.astype(jnp.bfloat16)


def set_ends(values, rng, least, largest):
    place = [jax.random.randint(jax.random.fold_in(rng, axis), (), 0, length) for axis, length in enumerate(values.shape)]
    widest = values.shape.index(max(values.shape))
    neighbour = place[:widest] + [(place[widest] + 1) % values.shape[widest]] + place[widest + 1:]
    return values.at[tuple(place)].set(least).at[tuple(neighbour)].set(largest)


def block_scale(stream_key, shape, shards, low, high):
    level, own = 1.0, jax.random.fold_in(stream_key, 6)
    for dim, shards_of in shards:
        draws = jnp.exp(jax.random.uniform(jax.random.fold_in(own, dim), (shards_of,), jnp.float32, low / len(shards), high / len(shards)))
        level = level * jnp.repeat(draws, shape[dim] // shards_of).reshape([-1 if axis == dim else 1 for axis in range(len(shape))])
    return level


def profile(count, total, reach, lean):
    weights = [(1 << 20) // math.isqrt(standing ** lean) + 1 for standing in range(2, count + 1)]
    surplus, counts = total - reach - (count - 1), [1] * (count - 1)
    while surplus > 0:
        candidates = [i for i in range(count - 1) if counts[i] < reach]
        whole, left = sum([weights[i] for i in candidates]), surplus
        for i in candidates:
            more = min(reach - counts[i], max(1, left * weights[i] // whole), surplus)
            counts[i] = counts[i] + more
            surplus = surplus - more
    return np.array([reach] + counts)


def uneven_parts(key, count, total, reach, lean):
    if count == 2:
        one = jax.random.randint(key, (), max(1, total - reach), min(reach, total - 1) + 1)
        return jnp.stack([one, total - one])
    tallies = jnp.asarray(profile(count, total, reach, lean), jnp.int32)
    pairs = (count - 1) // 2
    giver, sink = tallies[1:1 + 2 * pairs:2], tallies[2:2 + 2 * pairs:2]
    room = jnp.minimum(giver - 1, reach - sink)
    moved = jax.random.randint(jax.random.fold_in(key, 1), (pairs,), 0, 1 << 20) % (room + 1)
    tallies = tallies.at[1:1 + 2 * pairs:2].set(giver - moved).at[2:2 + 2 * pairs:2].set(sink + moved)
    return tallies[jax.random.permutation(jax.random.fold_in(key, 2), count)]


def deal_out(rng, own, number, rows, number_of, top, most, slope):
    order = jax.random.permutation(rng, number_of)
    heavy_load, usual = shares(number_of, rows * top, most, slope, True), shares(number_of, rows * top, most, slope, False)
    places = jnp.arange(number_of)

    def named(tallies, rotation):
        used = int((tallies > 0).sum())
        fixed = max(1, used // 4)
        moved = fixed + (places - fixed + rotation * (used - fixed)) % max(1, number_of - fixed)
        return jnp.zeros((number_of,), jnp.int32).at[order[jnp.where(places < fixed, places, moved)]].set(jnp.asarray(tallies, jnp.int32))

    tallies = jnp.where(number % 4 == 0, named(heavy_load, number // 4), named(usual, number - number // 4 - 1))
    mixed = jax.random.permutation(jax.random.fold_in(own, 3), number_of)
    donor, receiver = mixed[0:number_of // 2 * 2:2], mixed[1:number_of // 2 * 2:2]
    room = jnp.minimum(tallies[donor] - 1, most - tallies[receiver]) // 2
    room = jnp.where((donor == order[0]) | (receiver == order[0]) | (tallies[receiver] == 0), 0, jnp.maximum(room, 0))
    moved = jax.random.randint(jax.random.fold_in(own, 4), (number_of // 2,), 0, 1 << 20) % (room + 1)
    tallies = tallies.at[donor].add(-moved).at[receiver].add(moved)
    items = jnp.searchsorted(jnp.cumsum(tallies), jnp.arange(rows * top), side="right").astype(jnp.int32)
    grid = items.reshape(top, rows).T
    grid = grid[jax.random.permutation(jax.random.fold_in(own, 1), rows)]
    rotation = jax.random.randint(jax.random.fold_in(own, 2), (rows, 1), 0, top)
    return jnp.take_along_axis(grid, (jnp.arange(top)[None, :] + rotation) % top, axis=1)


def shares(count, total, bound, lean, full):
    portions = [(1 << 20) // math.isqrt(standing ** lean) + 1 for standing in range(1, count + 1)]
    largest = bound if full else min(bound, max(-(-total // count), total * portions[0] // sum(portions)))
    least = 1 if total - largest >= count - 1 else 0
    counts, rest = [largest] + [least] * (count - 1), total - largest - least * (count - 1)
    while rest > 0:
        candidates = [i for i in range(1, count) if counts[i] < largest] or [i for i in range(1, count) if counts[i] < bound]
        whole, budget = sum([portions[i] for i in candidates]), rest
        for i in candidates:
            extra = min(bound - counts[i], max(1, budget * portions[i] // whole), rest)
            counts[i] = counts[i] + extra
            rest = rest - extra
    return np.array(counts)


def centred(own_key, dims, deviation, limit, pieces=(), held_as=jnp.bfloat16):
    loudness = block_scale(own_key, dims, pieces, -0.22, 0.18) if pieces else 1.0
    array = jax.random.normal(own_key, dims, jnp.float32) * deviation * loudness
    return jnp.minimum(jnp.maximum(array, -limit), limit).astype(held_as)


def setup_inputs(seed: int = 0, part: int = 0) -> dict:
    seeds = jax.random.split(jax.random.key(seed), 14)
    part_splits = jax.random.split(jax.random.fold_in(seeds[13], part), 14)
    vis_query = draw_vis_query(jax.random.fold_in(jax.random.fold_in(seeds[13], part), 71), part)
    vis_keyvalue = draw_vis_keyvalue(jax.random.fold_in(jax.random.fold_in(seeds[13], part), 71), part)
    vis_residual = centred(part_splits[2], (PATCHES, VIS_WIDTH), 0.3, 4.0, ((0, 16),))
    vis_out_weight = centred(seeds[3], (VIS_WIDTH, VIS_WIDTH), VIS_WIDTH ** -0.5, 0.15625, ((0, 16),))
    vis_out_bias = centred(seeds[4], (VIS_WIDTH,), 0.3, 4.0, (), jnp.float32)
    image_units = uneven_parts(part_splits[5], IMAGES, UNITS, UNITS_DEV // 2, 2).astype(jnp.int32)
    text_embed = centred(part_splits[6], (TEXT, LM_WIDTH), 1.0, 6.0, ((0, 16),))
    lm_gain = jnp.clip(1.0 + 0.18 * jax.random.normal(seeds[7], (LM_WIDTH,), jnp.float32), 0.1, 1.9)
    lm_kv_weight = centred(seeds[8], (LM_WIDTH, KV_WIDTH), LM_WIDTH ** -0.5, 0.078125, ((1, 16),))
    lm_kv_bias = centred(seeds[9], (KV_WIDTH,), 0.5, 6.0, (), jnp.float32)
    text_positions = set_ends(jax.random.randint(part_splits[10], (TEXT,), 0, POS_LIMIT), jax.random.fold_in(part_splits[10], 1), 0, POS_LIMIT - 1).astype(jnp.int32)
    image_destination_keys = jax.random.split(jax.random.fold_in(part_splits[11], 1), UNITS // UNITS_DEV)
    image_destination_turns = jax.random.permutation(jax.random.fold_in(part_splits[11], 3), UNITS // UNITS_DEV)
    image_destination = jax.vmap(lambda own, number: deal_out(jax.random.fold_in(part_splits[11], 2), own, number, UNITS_DEV, DESTS, 1, CAP, 2))(image_destination_keys, image_destination_turns).reshape((UNITS, 1))
    image_positions = set_ends(jax.random.randint(part_splits[12], (3, IMG_SLOTS), 0, POS_LIMIT), jax.random.fold_in(part_splits[12], 1), 0, POS_LIMIT - 1).astype(jnp.int32)
    return dict(vis_query=vis_query, vis_keyvalue=vis_keyvalue, vis_residual=vis_residual, vis_out_weight=vis_out_weight, vis_out_bias=vis_out_bias, image_units=image_units, text_embed=text_embed, lm_gain=lm_gain, lm_kv_weight=lm_kv_weight, lm_kv_bias=lm_kv_bias, text_positions=text_positions, image_destination=image_destination, image_positions=image_positions)


norm_epsilon = 1e-06
rope_base = 1000000.0

def segment_ids(global_index, bounds):
    return lax.optimization_barrier(jnp.sum((global_index[:, None] >= bounds[None, :]).astype(jnp.int32), axis=1)) - 1

def rms_scale(rows, gain):
    values = rows.astype(jnp.float32)
    mean_square = lax.optimization_barrier(jnp.mean(values * values, axis=1, keepdims=True))
    return (values * lax.rsqrt(mean_square + norm_epsilon) * gain).astype(jnp.bfloat16)

def rotate_keys(values, bias, positions):
    shifted = values + bias
    row_count = shifted.shape[0]
    kv_half = shifted.shape[1] // 2
    half_size = LM_HEAD // 2
    key_part = shifted[:, :kv_half].reshape(row_count, KV_HEADS, LM_HEAD)
    lower_half = key_part[:, :, :half_size]
    upper_half = key_part[:, :, half_size:]
    index_pair = jnp.arange(half_size, dtype=jnp.int32)
    frequency = jnp.power(jnp.float32(rope_base), -2.0 * index_pair.astype(jnp.float32) / LM_HEAD)
    section = (index_pair >= half_size // 4).astype(jnp.int32) + (index_pair >= half_size // 4 + 3 * half_size // 8).astype(jnp.int32)
    places = positions.astype(jnp.float32)
    chosen = jnp.zeros((row_count, half_size), jnp.float32)
    for axis_number in range(3):
        chosen = chosen + places[axis_number][:, None] * (section == axis_number).astype(jnp.float32)[None, :]
    angles = chosen * frequency[None, :]
    cosine = jnp.cos(angles)[:, None, :]
    sine_part = jnp.sin(angles)[:, None, :]
    turned = jnp.concatenate([lower_half * cosine - upper_half * sine_part, upper_half * cosine + lower_half * sine_part], axis=2)
    return jnp.concatenate([turned.reshape(row_count, kv_half), shifted[:, kv_half:]], axis=1).astype(jnp.bfloat16)

def reference(vis_query, vis_keyvalue, vis_residual, vis_out_weight, vis_out_bias, image_units, text_embed, lm_gain, lm_kv_weight, lm_kv_bias, text_positions, image_destination, image_positions):
    head_size = VIS_WIDTH // VIS_HEADS
    half_window = PATCH_DEV // 2
    bounds = jnp.concatenate([jnp.zeros((1,), jnp.int32), jnp.cumsum(4 * image_units).astype(jnp.int32)])
    margin = jnp.zeros((2, half_window, VIS_WIDTH), jnp.bfloat16)
    padded = jnp.concatenate([margin, vis_keyvalue, margin], axis=1)
    score_scale = 1.0 / math.sqrt(head_size)

    def one_block(block):
        offset = (block * PATCH_DEV).astype(jnp.int32)
        queries = lax.dynamic_slice_in_dim(vis_query, offset, PATCH_DEV, 0).astype(jnp.float32).reshape(PATCH_DEV, VIS_HEADS, head_size)
        nearby = lax.dynamic_slice_in_dim(padded, offset, 2 * PATCH_DEV, 1).astype(jnp.float32).reshape(2, 2 * PATCH_DEV, VIS_HEADS, head_size)
        query_ids = segment_ids(offset + jnp.arange(PATCH_DEV, dtype=jnp.int32), bounds)
        key_ids = segment_ids(offset - half_window + jnp.arange(2 * PATCH_DEV, dtype=jnp.int32), bounds)
        allowed = query_ids[:, None] == key_ids[None, :]
        scores = jnp.einsum('qhd,khd->hqk', queries, nearby[0]) * score_scale
        scores = jnp.where(allowed[None], scores, -1e+30)
        row_max = lax.optimization_barrier(jnp.max(scores, axis=2, keepdims=True))
        shifted = jnp.exp(scores - row_max)
        weights = (shifted / lax.optimization_barrier(jnp.sum(shifted, axis=2, keepdims=True))).astype(jnp.bfloat16)
        weights = lax.optimization_barrier(weights).astype(jnp.float32)
        mixed = jnp.einsum('hqk,khd->qhd', weights, nearby[1])
        return mixed.astype(jnp.bfloat16).reshape(PATCH_DEV, VIS_WIDTH)
    attended = lax.map(one_block, jnp.arange(N_TOK, dtype=jnp.int32)).reshape(PATCHES, VIS_WIDTH)
    projected = jnp.dot(attended, vis_out_weight, preferred_element_type=jnp.float32)
    vis_hidden = (projected + vis_out_bias + vis_residual.astype(jnp.float32)).astype(jnp.bfloat16)
    merged = vis_hidden.reshape(UNITS, LM_WIDTH)
    image_rows = jnp.dot(rms_scale(merged, lm_gain), lm_kv_weight, preferred_element_type=jnp.float32)
    target = image_destination[:, 0].reshape(N_TOK, UNITS_DEV)
    same_target = target[:, :, None] == target[:, None, :]
    earlier = jnp.arange(UNITS_DEV, dtype=jnp.int32)[None, :] < jnp.arange(UNITS_DEV, dtype=jnp.int32)[:, None]
    slot_rank = lax.optimization_barrier(jnp.sum((same_target & earlier[None]).astype(jnp.int32), axis=2))
    source = jnp.arange(N_TOK, dtype=jnp.int32)[:, None]
    slot_index = (target * SLOTS_DEV + source * CAP + slot_rank).reshape(UNITS).astype(jnp.int32)
    image_values = jnp.zeros((IMG_SLOTS, KV_WIDTH), jnp.float32).at[slot_index].set(image_rows)
    image_cache = rotate_keys(image_values, lm_kv_bias, image_positions)
    text_values = jnp.dot(rms_scale(text_embed, lm_gain), lm_kv_weight, preferred_element_type=jnp.float32)
    text_cache = rotate_keys(text_values, lm_kv_bias, jnp.broadcast_to(text_positions[None, :], (3, TEXT)))
    return (text_cache, image_cache)
```

```python
import functools
import math

import jax
import jax.numpy as jnp
from jax import lax
from jax.experimental import pallas as pl
from jax.experimental.pallas import tpu as pltpu
from jax.sharding import PartitionSpec as P

VIS_HEADS = 16
KV_HEADS = 8
LM_HEAD = 128


norm_epsilon = 1e-06
rope_base = 1000000.0


def with_halo(block, sides, width):
    for axis, dim in sides:
        count = lax.axis_size(axis)
        forward = [(i, i + 1) for i in range(count - 1)]
        backward = [(target, source) for source, target in forward]
        low = lax.ppermute(
            lax.slice_in_dim(block, block.shape[dim] - width, None, axis=dim), axis, forward
        )
        high = lax.ppermute(lax.slice_in_dim(block, 0, width, axis=dim), axis, backward)
        block = jnp.concatenate([low, block, high], axis=dim)
    return block


def segment_ids(global_index, bounds):
    return jnp.sum((global_index[:, None] >= bounds[None, :]).astype(jnp.int32), axis=1) - 1


def rms_scale(rows, gain):
    values = rows.astype(jnp.float32)
    mean_square = jnp.mean(values * values, axis=1, keepdims=True)
    return (values * lax.rsqrt(mean_square + norm_epsilon) * gain).astype(jnp.bfloat16)


def rotation_tables(positions):
    half_size = LM_HEAD // 2
    index_pair = jnp.arange(half_size, dtype=jnp.int32)
    frequency = jnp.power(jnp.float32(rope_base), -2.0 * index_pair.astype(jnp.float32) / LM_HEAD)
    section = (index_pair >= half_size // 4).astype(jnp.int32) + (
        index_pair >= half_size // 4 + 3 * half_size // 8
    ).astype(jnp.int32)
    places = positions.astype(jnp.float32)
    chosen = jnp.zeros((positions.shape[1], half_size), jnp.float32)
    for axis_number in range(3):
        chosen = (
            chosen
            + places[axis_number][:, None] * (section == axis_number).astype(jnp.float32)[None, :]
        )
    angles = chosen * frequency[None, :]
    return jnp.cos(angles), jnp.sin(angles)


def rotate_keys(values, bias, positions):
    shifted = values + bias
    row_count = shifted.shape[0]
    kv_half = shifted.shape[1] // 2
    half_size = LM_HEAD // 2
    key_part = shifted[:, :kv_half].reshape(row_count, KV_HEADS, LM_HEAD)
    lower_half = key_part[:, :, :half_size]
    upper_half = key_part[:, :, half_size:]
    cosine, sine_part = rotation_tables(positions)
    cosine, sine_part = cosine[:, None, :], sine_part[:, None, :]
    turned = jnp.concatenate(
        [
            lower_half * cosine - upper_half * sine_part,
            upper_half * cosine + lower_half * sine_part,
        ],
        axis=2,
    )
    return jnp.concatenate(
        [turned.reshape(row_count, kv_half), shifted[:, kv_half:]], axis=1
    ).astype(jnp.bfloat16)


def head_attention(query_head, key_head, value_head, allowed, score_scale):
    scores = (
        jnp.einsum("qd,kd->qk", query_head, key_head, preferred_element_type=jnp.float32)
        * score_scale
    )
    scores = jnp.where(allowed, scores, -1e30)
    row_max = jnp.max(scores, axis=1, keepdims=True)
    shifted = jnp.exp(scores - row_max)
    weights = (shifted / jnp.sum(shifted, axis=1, keepdims=True)).astype(jnp.bfloat16)
    return jnp.dot(weights, value_head, preferred_element_type=jnp.float32).astype(jnp.bfloat16)


def project_rows(normed, kv_weight):
    return jnp.dot(
        normed,
        lax.all_gather(kv_weight, "tok", axis=1, tiled=True),
        preferred_element_type=jnp.float32,
    )


def ranks_of(target):
    unit_count = target.shape[0]
    same_target = target[:, None] == target[None, :]
    earlier = (
        jnp.arange(unit_count, dtype=jnp.int32)[None, :]
        < jnp.arange(unit_count, dtype=jnp.int32)[:, None]
    )
    return jnp.sum((same_target & earlier).astype(jnp.int32), axis=1)


def per_device_gathered(
    vis_query,
    vis_keyvalue,
    vis_residual,
    vis_out_weight,
    vis_out_bias,
    image_units,
    text_embed,
    lm_gain,
    lm_kv_weight,
    lm_kv_bias,
    text_positions,
    image_destination,
    image_positions,
):
    patch_count, vis_width = vis_query.shape
    head_size = vis_width // VIS_HEADS
    half_window = patch_count // 2
    device_count = lax.axis_size("tok")
    device_index = lax.axis_index("tok")
    nearby = with_halo(vis_keyvalue, (("tok", 1),), half_window)
    bounds = jnp.concatenate([jnp.zeros((1,), jnp.int32), jnp.cumsum(4 * image_units)])
    offset = device_index * patch_count
    query_ids = segment_ids(offset + jnp.arange(patch_count, dtype=jnp.int32), bounds)
    key_ids = segment_ids(
        offset - half_window + jnp.arange(2 * patch_count, dtype=jnp.int32), bounds
    )
    allowed = query_ids[:, None] == key_ids[None, :]
    score_scale = 1.0 / math.sqrt(head_size)
    query_heads = vis_query.reshape(patch_count, VIS_HEADS, head_size).transpose(1, 0, 2)
    key_heads = nearby[0].reshape(2 * patch_count, VIS_HEADS, head_size).transpose(1, 0, 2)
    value_heads = nearby[1].reshape(2 * patch_count, VIS_HEADS, head_size).transpose(1, 0, 2)
    attended = lax.map(
        lambda pieces: head_attention(pieces[0], pieces[1], pieces[2], allowed, score_scale),
        (query_heads, key_heads, value_heads),
    )
    attended = attended.transpose(1, 0, 2).reshape(patch_count, vis_width)
    projected = jnp.dot(
        attended,
        lax.all_gather(vis_out_weight, "tok", axis=0, tiled=True),
        preferred_element_type=jnp.float32,
    )
    vis_hidden = (projected + vis_out_bias + vis_residual.astype(jnp.float32)).astype(jnp.bfloat16)
    merged = vis_hidden.reshape(patch_count // 4, 4 * vis_width)
    target = image_destination[:, 0]
    slot_count = image_positions.shape[1]
    capacity = slot_count // device_count
    slot_index = target * capacity + ranks_of(target)
    text_count = text_embed.shape[0]
    kv_width = lm_kv_bias.shape[0]
    normed = rms_scale(jnp.concatenate([text_embed, merged], axis=0), lm_gain)
    projected_rows = project_rows(normed, lm_kv_weight)
    text_values = projected_rows[:text_count]
    outgoing = (
        jnp.zeros((slot_count, kv_width), jnp.float32)
        .at[slot_index]
        .set(projected_rows[text_count:])
    )
    image_values = lax.all_to_all(outgoing, "tok", split_axis=0, concat_axis=0, tiled=True)
    text_cache = rotate_keys(
        text_values, lm_kv_bias, jnp.broadcast_to(text_positions[None, :], (3, text_count))
    )
    image_cache = rotate_keys(image_values, lm_kv_bias, image_positions)
    return (text_cache, image_cache)


def call_kernel(body, outs, *args, scalars=(), scratch=(), cost=None):
    flops, moved = cost if cost else (0, 0)
    return pl.pallas_call(
        body,
        out_shape=outs,
        in_specs=[pl.BlockSpec(memory_space=pltpu.SMEM)] * len(scalars)
        + [pl.BlockSpec(memory_space=pltpu.VMEM)] * len(args),
        out_specs=jax.tree.map(lambda _: pl.BlockSpec(memory_space=pltpu.VMEM), outs),
        scratch_shapes=list(scratch),
        cost_estimate=pl.CostEstimate(flops=flops, bytes_accessed=moved, transcendentals=0),
        compiler_params=pltpu.CompilerParams(vmem_limit_bytes=56 << 20),
    )(*scalars, *args)


def attention_body(
    place, query, own, low, high, units_row, units_col, attended, *, head_size, window
):
    patch_count, vis_width = query.shape
    half = patch_count // 2
    count = units_row.shape[1]
    first = place[0] * patch_count
    wide = lax.broadcasted_iota(jnp.int32, (count, count), 0)
    across = lax.broadcasted_iota(jnp.int32, (count, count), 1)
    row_sums = jnp.where(wide <= across, units_col[...], 0)
    ends_row = 4 * jnp.sum(row_sums, axis=0, keepdims=True)
    col_sums = jnp.where(across <= wide, units_row[...], 0)
    ends_col = 4 * jnp.sum(col_sums, axis=1, keepdims=True)
    patch = first + lax.broadcasted_iota(jnp.int32, (patch_count, 1), 0)
    query_ids = jnp.sum((patch >= ends_row).astype(jnp.int32), axis=1, keepdims=True)
    near = first - half + lax.broadcasted_iota(jnp.int32, (1, 2 * patch_count), 1)
    key_ids = jnp.sum((near >= ends_col).astype(jnp.int32), axis=0, keepdims=True)
    key_ids = jnp.where(near < 0, -1, key_ids)
    score_scale = 1.0 / math.sqrt(head_size)
    allowed = [
        query_ids[b * half : (b + 1) * half] == key_ids[:, b * half : (b + 3) * half]
        for b in range(2)
    ]
    sides = (low, high)
    contract = (((1,), (1,)), ((), ()))

    def one_head(head, carry):
        begin = pl.multiple_of(
            jnp.minimum((head * head_size) // LM_HEAD * LM_HEAD, vis_width - window), LM_HEAD
        )
        columns = pl.ds(begin, window)
        lane = lax.broadcasted_iota(jnp.int32, (1, window), 1) + begin
        mine = (lane >= head * head_size) & (lane < (head + 1) * head_size)
        picked = jnp.where(mine, query[:, columns], 0)
        middle = lax.dot_general(
            picked, own[0, :, columns], contract, preferred_element_type=jnp.float32
        )
        for b in range(2):
            rows = slice(b * half, (b + 1) * half)
            edge = lax.dot_general(
                picked[rows], sides[b][0, :, columns], contract, preferred_element_type=jnp.float32
            )
            parts = [edge, middle[rows]] if b == 0 else [middle[rows], edge]
            scores = jnp.concatenate(parts, axis=1) * score_scale
            scores = jnp.where(allowed[b], scores, -1e30)
            shifted = jnp.exp(scores - jnp.max(scores, axis=1, keepdims=True))
            weights = (shifted / jnp.sum(shifted, axis=1, keepdims=True)).astype(jnp.bfloat16)
            split = half if b == 0 else 2 * half
            pieces = (low[1, :, columns], own[1, :, columns])
            if b == 1:
                pieces = (own[1, :, columns], high[1, :, columns])
            mixed = jnp.dot(
                weights[:, :split], pieces[0], preferred_element_type=jnp.float32
            ) + jnp.dot(weights[:, split:], pieces[1], preferred_element_type=jnp.float32)
            attended[rows, columns] = jnp.where(
                mine, mixed.astype(jnp.bfloat16), attended[rows, columns]
            )
        return carry

    lax.fori_loop(0, vis_width // head_size, one_head, 0)


def normed_rows(values, gain):
    mean_square = jnp.mean(values * values, axis=1, keepdims=True)
    return (values * lax.rsqrt(mean_square + norm_epsilon) * gain).astype(jnp.bfloat16)


def norm_body(rows, gain, normed):
    normed[...] = normed_rows(rows[...].astype(jnp.float32), gain[...])


def hidden_body(heads, attended, *refs):
    pieces, (bias, residual, gain, normed, weight, hidden) = refs[:-6], refs[-6:]
    depth = pieces[0].shape[1]
    for number, piece in enumerate(pieces):
        for part in range(piece.shape[0]):
            start = pl.multiple_of(heads[number * piece.shape[0] + part] * depth, 16)
            weight[pl.ds(start, depth), :] = piece[part]
    total = jnp.dot(attended[...], weight[...], preferred_element_type=jnp.float32)
    total = total + bias[...] + residual[...].astype(jnp.float32)
    total = total.astype(jnp.bfloat16).astype(jnp.float32)
    tiles, units = hidden.shape[0], hidden.shape[1] // 4
    for tile in range(tiles):
        hidden[tile] = total[:, tile * LM_HEAD : (tile + 1) * LM_HEAD]
    merged = jnp.concatenate(
        [
            hidden[tile, pl.ds(part, units, stride=4), :]
            for part in range(4)
            for tile in range(tiles)
        ],
        axis=1,
    )
    normed[...] = normed_rows(merged, gain[...])


def pair_product(side, rows, pieces):
    if len(pieces) == 2:
        weight = jnp.concatenate([pieces[0][...], pieces[1][...]], axis=1)
        return jnp.dot(rows[...], weight, preferred_element_type=jnp.float32)
    depth = pieces[0].shape[0]
    total = None
    for number in range(2):
        begin = side if number == 0 else 1 - side
        columns = pl.ds(pl.multiple_of(begin * depth, LM_HEAD), depth)
        weight = jnp.concatenate(
            [pieces[2 * number][...], pieces[2 * number + 1][...]], axis=1
        )
        term = jnp.dot(rows[:, columns], weight, preferred_element_type=jnp.float32)
        total = term if total is None else total + term
    return total


def text_body(meta, own, sibling, *refs):
    pieces, (bias, cosine, sine, out_own, out_sibling) = refs[:-5], refs[-5:]
    count = own.shape[0]
    for number, (rows, out) in enumerate(((own, out_own), (sibling, out_sibling))):
        values = pair_product(meta[0], rows, pieces)
        span = slice(number * count, (number + 1) * count)
        for part in range(2):
            block = meta[1 + part]
            key = block < KV_HEADS
            shifted = values[:, part * LM_HEAD : (part + 1) * LM_HEAD] + bias[block]
            turn = jnp.where(key, cosine[span], 1.0)
            cross = jnp.where(key, sine[span], 0.0)
            turned = shifted * turn + pltpu.roll(shifted, LM_HEAD // 2, 1) * cross
            out[part] = turned.astype(jnp.bfloat16)


def image_body(meta, own, sibling, place, *refs, groups):
    pieces, out = refs[:-1], refs[-1]
    begin = 0
    for number, size in enumerate(groups):
        mine = pieces[begin : begin + size]
        begin += size
        values = jnp.concatenate(
            [pair_product(meta[0], rows, mine) for rows in (own, sibling)], axis=0
        ).astype(jnp.bfloat16)
        placed = jnp.dot(place[...], values, preferred_element_type=jnp.float32)
        out[:, number * 2 * LM_HEAD : (number + 1) * 2 * LM_HEAD] = placed.astype(jnp.bfloat16)


def text_cache_body(blocks, *refs):
    pieces, out = refs[:-1], refs[-1]
    for number, piece in enumerate(pieces):
        for part in range(2):
            begin = pl.multiple_of(blocks[2 * number + part] * LM_HEAD, LM_HEAD)
            out[:, pl.ds(begin, LM_HEAD)] = piece[part]


def image_cache_body(*refs, orders):
    arrivals, (bias, cosine, sine, out) = refs[:-4], refs[-4:]
    device_count = arrivals[0].shape[0]
    depth = arrivals[0].shape[1]
    for source in range(device_count):
        rows = slice(source // 2 * depth, (source // 2 + 1) * depth)
        place = 0
        for arrival in arrivals:
            for part in range(arrival.shape[2] // LM_HEAD):
                block = orders[source][place]
                place += 1
                shifted = (
                    arrival[source, :, part * LM_HEAD : (part + 1) * LM_HEAD].astype(jnp.float32)
                    + bias[block]
                )
                if block < KV_HEADS:
                    shifted = (
                        shifted * cosine[rows]
                        + pltpu.roll(shifted, LM_HEAD // 2, 1) * sine[rows]
                    )
                out[rows, block * LM_HEAD : (block + 1) * LM_HEAD] = shifted.astype(jnp.bfloat16)


def full_tables(positions):
    cosine, sine = rotation_tables(positions)
    return jnp.concatenate([cosine, cosine], axis=1), jnp.concatenate([-sine, sine], axis=1)


def per_device(
    vis_query,
    vis_keyvalue,
    vis_residual,
    vis_out_weight,
    vis_out_bias,
    image_units,
    text_embed,
    lm_gain,
    lm_kv_weight,
    lm_kv_bias,
    text_positions,
    image_destination,
    image_positions,
):
    bf16, f32 = jnp.bfloat16, jnp.float32
    patch_count, vis_width = vis_query.shape
    head_size = vis_width // VIS_HEADS
    half_window = patch_count // 2
    count = lax.axis_size("tok")
    rings = count // 4
    me = lax.axis_index("tok")
    side = lax.axis_index("groups")
    text_count, lm_width = text_embed.shape
    units = image_destination.shape[0]
    slot_count = image_positions.shape[1]
    capacity = slot_count // count

    sibling = [(i, i ^ 1) for i in range(count)]
    across = [(i, i ^ 2) for i in range(count)]

    def ring(value, steps=1):
        return lax.ppermute(value, "tok", [(i, (i + 4 * steps) % count) for i in range(count)])

    def swap(value):
        return lax.ppermute(value, "groups", [(0, 1), (1, 0)])

    forward = [(i, i + 1) for i in range(count - 1)]
    backward = [(i + 1, i) for i in range(count - 1)]
    low = lax.ppermute(vis_keyvalue[:, patch_count - half_window :], "tok", forward)
    high = lax.ppermute(vis_keyvalue[:, :half_window], "tok", backward)

    half_depth = lm_width // 2
    half = lax.dynamic_slice_in_dim(lm_kv_weight, side * half_depth, half_depth, 0)
    ring_halves, side_halves = [half], []
    for _ in range(rings - 1):
        ring_halves.append(ring(ring_halves[-1]))
    whole_across = lax.ppermute(lm_kv_weight, "tok", across)
    for step in range(1, rings):
        side_halves.append(lax.ppermute(ring_halves[step], "tok", across))
    groups = [[lm_kv_weight, whole_across]]
    for step in range(1, rings):
        mine = [ring_halves[step], side_halves[step - 1]]
        groups.append(mine + [swap(piece) for piece in mine])

    rows_across = lax.ppermute(vis_out_weight, "tok", across)
    row_pair = jnp.stack([vis_out_weight, rows_across])
    row_pairs = [row_pair] + [ring(row_pair, step) for step in range(1, rings)]
    row_stack = jnp.concatenate(row_pairs, axis=0)
    row_other = lax.ppermute(row_stack, "tok", sibling)

    target = image_destination[:, 0]
    numbers = jnp.concatenate([text_positions, target])
    other_numbers = lax.ppermute(numbers, "tok", sibling)

    gain = lm_gain[None, :]
    normed_own = call_kernel(
        norm_body,
        jax.ShapeDtypeStruct((text_count, lm_width), bf16),
        text_embed,
        gain,
        cost=(text_count * lm_width * 8, 4 * text_count * lm_width),
    )
    normed_other = lax.ppermute(normed_own, "tok", sibling)

    attended = call_kernel(
        functools.partial(attention_body, head_size=head_size, window=2 * LM_HEAD),
        jax.ShapeDtypeStruct((patch_count, vis_width), bf16),
        vis_query,
        vis_keyvalue,
        low,
        high,
        image_units[None, :],
        image_units[:, None],
        scalars=(me[None].astype(jnp.int32),),
        cost=(patch_count * patch_count * vis_width * 24, 8 * patch_count * vis_width),
    )

    depth = vis_out_weight.shape[0]
    core, line, floor = me % 2, me // 2 % 2, me // 4
    floors = [(floor - step) % rings for step in range(rings)]
    own_blocks = [f * 4 + (line ^ part) * 2 + core for f in floors for part in range(2)]
    other_blocks = [f * 4 + (line ^ part) * 2 + 1 - core for f in floors for part in range(2)]
    normed_image = call_kernel(
        hidden_body,
        jax.ShapeDtypeStruct((patch_count // 4, 4 * vis_width), bf16),
        attended,
        row_stack,
        row_other,
        vis_out_bias[None, :],
        vis_residual,
        gain,
        scalars=(jnp.stack(own_blocks + other_blocks).astype(jnp.int32),),
        scratch=[
            pltpu.VMEM((count * depth, vis_width), bf16),
            pltpu.VMEM((vis_width // LM_HEAD, patch_count, LM_HEAD), f32),
        ],
        cost=(2 * patch_count * vis_width * vis_width, 2 * vis_width * vis_width),
    )
    normed_image_other = lax.ppermute(normed_image, "tok", sibling)

    other_target = other_numbers[text_count:]
    slot_own = target * (2 * capacity) + core * capacity + ranks_of(target)
    slot_other = other_target * (2 * capacity) + (1 - core) * capacity + ranks_of(other_target)
    slots = jnp.concatenate([slot_own, slot_other])
    place = (
        jnp.arange(2 * slot_count, dtype=jnp.int32)[:, None] == slots[None, :]
    ).astype(bf16)

    both_positions = jnp.concatenate([text_positions, other_numbers[:text_count]])
    cosine, sine = full_tables(jnp.broadcast_to(both_positions[None, :], (3, 2 * text_count)))
    bias = lm_kv_bias.reshape(-1, 1, LM_HEAD)

    side_int = side.astype(jnp.int32)
    blocks_own, blocks_other = [], []
    for number, group in enumerate(groups):
        meta = jnp.stack([side_int] + own_blocks[2 * number : 2 * number + 2]).astype(jnp.int32)
        kept, given = call_kernel(
            text_body,
            [jax.ShapeDtypeStruct((2, text_count, LM_HEAD), bf16)] * 2,
            normed_own,
            normed_other,
            *group,
            bias,
            cosine,
            sine,
            scalars=(meta,),
            cost=(8 * text_count * lm_width * LM_HEAD, 4 * text_count * lm_width),
        )
        blocks_own.append(kept)
        blocks_other.append(lax.ppermute(given, "tok", sibling))

    arrivals = []
    for chosen in (groups[:-1], groups[-1:]):
        outgoing = call_kernel(
            functools.partial(image_body, groups=[len(group) for group in chosen]),
            jax.ShapeDtypeStruct((2 * slot_count, 2 * LM_HEAD * len(chosen)), bf16),
            normed_image,
            normed_image_other,
            place,
            *[piece for group in chosen for piece in group],
            scalars=(side_int[None],),
            cost=(
                8 * units * lm_width * LM_HEAD * len(chosen),
                4 * lm_width * LM_HEAD * len(chosen),
            ),
        )
        arrived = lax.all_to_all(outgoing, "tok", split_axis=0, concat_axis=0, tiled=True)
        arrivals.append(arrived.reshape(count, 2 * capacity, -1))

    text_cache = call_kernel(
        text_cache_body,
        jax.ShapeDtypeStruct((text_count, count * LM_HEAD), bf16),
        *blocks_own,
        *blocks_other,
        scalars=(jnp.stack(own_blocks + other_blocks).astype(jnp.int32),),
    )
    orders = [
        [
            (source // 4 - step) % rings * 4 + (source // 2 % 2 ^ part) * 2 + source % 2
            for step in range(rings)
            for part in range(2)
        ]
        for source in range(count)
    ]
    image_cosine, image_sine = full_tables(image_positions)
    image_cache = call_kernel(
        functools.partial(image_cache_body, orders=orders),
        jax.ShapeDtypeStruct((slot_count, count * LM_HEAD), bf16),
        *arrivals,
        bias,
        image_cosine,
        image_sine,
    )
    return (text_cache, image_cache)


def solution(mesh):
    placed = (
        P(("groups", "tok"), None),
        P(None, ("groups", "tok"), None),
        P(("groups", "tok"), None),
        P("tok", None),
        P(),
        P("groups"),
        P(("groups", "tok"), None),
        P(),
        P(None, "tok"),
        P(),
        P(("groups", "tok")),
        P(("groups", "tok"), None),
        P(None, ("groups", "tok")),
    )

    def chosen(*args):
        weight, out_weight, slots = args[8], args[3], args[12].shape[1] // lax.axis_size("tok")
        fits = (
            weight.shape[1] == LM_HEAD
            and lax.axis_size("groups") == 2
            and lax.axis_size("tok") % 4 == 0
            and weight.shape[0] % (2 * LM_HEAD) == 0
            and out_weight.shape[0] % 16 == 0
            and slots % 8 == 0
        )
        return (per_device if fits else per_device_gathered)(*args)

    return jax.shard_map(
        chosen,
        mesh=mesh,
        in_specs=placed,
        out_specs=(P(("groups", "tok"), None), P(("groups", "tok"), None)),
        check_vma=False,
    )
```

```python
import functools
import math

import jax
import jax.numpy as jnp
from jax import lax
from jax.experimental import pallas as pl
from jax.experimental.pallas import tpu as pltpu
from jax.sharding import PartitionSpec as P


VIS_HEADS = 16
KV_HEADS = 8
LM_HEAD = 128


norm_epsilon = 1e-06
rope_base = 1000000.0


def with_halo(block, sides, width):
    for axis, dim in sides:
        count = lax.axis_size(axis)
        forward = [(i, i + 1) for i in range(count - 1)]
        backward = [(target, source) for source, target in forward]
        low = lax.ppermute(
            lax.slice_in_dim(block, block.shape[dim] - width, None, axis=dim), axis, forward
        )
        high = lax.ppermute(lax.slice_in_dim(block, 0, width, axis=dim), axis, backward)
        block = jnp.concatenate([low, block, high], axis=dim)
    return block


def segment_ids(global_index, bounds):
    return jnp.sum((global_index[:, None] >= bounds[None, :]).astype(jnp.int32), axis=1) - 1


def rms_scale(rows, gain):
    values = rows.astype(jnp.float32)
    mean_square = jnp.mean(values * values, axis=1, keepdims=True)
    return (values * lax.rsqrt(mean_square + norm_epsilon) * gain).astype(jnp.bfloat16)


def rotation_tables(positions):
    half_size = LM_HEAD // 2
    index_pair = jnp.arange(half_size, dtype=jnp.int32)
    frequency = jnp.power(jnp.float32(rope_base), -2.0 * index_pair.astype(jnp.float32) / LM_HEAD)
    section = (index_pair >= half_size // 4).astype(jnp.int32) + (
        index_pair >= half_size // 4 + 3 * half_size // 8
    ).astype(jnp.int32)
    places = positions.astype(jnp.float32)
    chosen = jnp.zeros((positions.shape[1], half_size), jnp.float32)
    for axis_number in range(3):
        chosen = (
            chosen
            + places[axis_number][:, None] * (section == axis_number).astype(jnp.float32)[None, :]
        )
    angles = chosen * frequency[None, :]
    return jnp.cos(angles), jnp.sin(angles)


def rotate_keys(values, bias, positions):
    shifted = values + bias
    row_count = shifted.shape[0]
    kv_half = shifted.shape[1] // 2
    half_size = LM_HEAD // 2
    key_part = shifted[:, :kv_half].reshape(row_count, KV_HEADS, LM_HEAD)
    lower_half = key_part[:, :, :half_size]
    upper_half = key_part[:, :, half_size:]
    cosine, sine_part = rotation_tables(positions)
    cosine, sine_part = cosine[:, None, :], sine_part[:, None, :]
    turned = jnp.concatenate(
        [
            lower_half * cosine - upper_half * sine_part,
            upper_half * cosine + lower_half * sine_part,
        ],
        axis=2,
    )
    return jnp.concatenate(
        [turned.reshape(row_count, kv_half), shifted[:, kv_half:]], axis=1
    ).astype(jnp.bfloat16)


def head_attention(query_head, key_head, value_head, allowed, score_scale):
    scores = (
        jnp.einsum("qd,kd->qk", query_head, key_head, preferred_element_type=jnp.float32)
        * score_scale
    )
    scores = jnp.where(allowed, scores, -1e30)
    row_max = jnp.max(scores, axis=1, keepdims=True)
    shifted = jnp.exp(scores - row_max)
    weights = (shifted / jnp.sum(shifted, axis=1, keepdims=True)).astype(jnp.bfloat16)
    return jnp.dot(weights, value_head, preferred_element_type=jnp.float32).astype(jnp.bfloat16)


def project_rows(normed, kv_weight):
    return jnp.dot(
        normed,
        lax.all_gather(kv_weight, "tok", axis=1, tiled=True),
        preferred_element_type=jnp.float32,
    )


def ranks_of(target):
    unit_count = target.shape[0]
    same_target = target[:, None] == target[None, :]
    earlier = (
        jnp.arange(unit_count, dtype=jnp.int32)[None, :]
        < jnp.arange(unit_count, dtype=jnp.int32)[:, None]
    )
    return jnp.sum((same_target & earlier).astype(jnp.int32), axis=1)


def per_device_gathered(
    vis_query,
    vis_keyvalue,
    vis_residual,
    vis_out_weight,
    vis_out_bias,
    image_units,
    text_embed,
    lm_gain,
    lm_kv_weight,
    lm_kv_bias,
    text_positions,
    image_destination,
    image_positions,
):
    patch_count, vis_width = vis_query.shape
    head_size = vis_width // VIS_HEADS
    half_window = patch_count // 2
    device_count = lax.axis_size("tok")
    device_index = lax.axis_index("tok")
    nearby = with_halo(vis_keyvalue, (("tok", 1),), half_window)
    bounds = jnp.concatenate([jnp.zeros((1,), jnp.int32), jnp.cumsum(4 * image_units)])
    offset = device_index * patch_count
    query_ids = segment_ids(offset + jnp.arange(patch_count, dtype=jnp.int32), bounds)
    key_ids = segment_ids(
        offset - half_window + jnp.arange(2 * patch_count, dtype=jnp.int32), bounds
    )
    allowed = query_ids[:, None] == key_ids[None, :]
    score_scale = 1.0 / math.sqrt(head_size)
    query_heads = vis_query.reshape(patch_count, VIS_HEADS, head_size).transpose(1, 0, 2)
    key_heads = nearby[0].reshape(2 * patch_count, VIS_HEADS, head_size).transpose(1, 0, 2)
    value_heads = nearby[1].reshape(2 * patch_count, VIS_HEADS, head_size).transpose(1, 0, 2)
    attended = lax.map(
        lambda pieces: head_attention(pieces[0], pieces[1], pieces[2], allowed, score_scale),
        (query_heads, key_heads, value_heads),
    )
    attended = attended.transpose(1, 0, 2).reshape(patch_count, vis_width)
    projected = jnp.dot(
        attended,
        lax.all_gather(vis_out_weight, "tok", axis=0, tiled=True),
        preferred_element_type=jnp.float32,
    )
    vis_hidden = (projected + vis_out_bias + vis_residual.astype(jnp.float32)).astype(jnp.bfloat16)
    merged = vis_hidden.reshape(patch_count // 4, 4 * vis_width)
    target = image_destination[:, 0]
    slot_count = image_positions.shape[1]
    capacity = slot_count // device_count
    slot_index = target * capacity + ranks_of(target)
    text_count = text_embed.shape[0]
    kv_width = lm_kv_bias.shape[0]
    normed = rms_scale(jnp.concatenate([text_embed, merged], axis=0), lm_gain)
    projected_rows = project_rows(normed, lm_kv_weight)
    text_values = projected_rows[:text_count]
    outgoing = (
        jnp.zeros((slot_count, kv_width), jnp.float32)
        .at[slot_index]
        .set(projected_rows[text_count:])
    )
    image_values = lax.all_to_all(outgoing, "tok", split_axis=0, concat_axis=0, tiled=True)
    text_cache = rotate_keys(
        text_values, lm_kv_bias, jnp.broadcast_to(text_positions[None, :], (3, text_count))
    )
    image_cache = rotate_keys(image_values, lm_kv_bias, image_positions)
    return (text_cache, image_cache)


def call_kernel(body, outs, *args, specs=None, scratch=(), cost=None, limit=10):
    flops, moved = cost if cost else (0, 0)
    return pl.pallas_call(
        body,
        out_shape=outs,
        grid=(1,) if specs else (),
        in_specs=specs or [pl.BlockSpec(memory_space=pltpu.VMEM)] * len(args),
        out_specs=jax.tree.map(lambda _: pl.BlockSpec(memory_space=pltpu.VMEM), outs),
        scratch_shapes=list(scratch),
        cost_estimate=pl.CostEstimate(flops=flops, bytes_accessed=moved, transcendentals=0),
        compiler_params=pltpu.CompilerParams(vmem_limit_bytes=limit << 20),
    )(*args)


def attention_body(query, own, low, high, units, attended, *, head_size, window):
    patch_count, width = query.shape
    half = patch_count // 2
    count = units.shape[1]
    first = lax.axis_index("tok") * patch_count
    wide = lax.broadcasted_iota(jnp.int32, (count, count), 0)
    across = lax.broadcasted_iota(jnp.int32, (count, count), 1)
    units_col = jnp.sum(jnp.where(wide == across, units[...], 0), axis=1, keepdims=True)
    ends_row = 4 * jnp.sum(jnp.where(wide <= across, units_col, 0), axis=0, keepdims=True)
    ends_col = 4 * jnp.sum(jnp.where(across <= wide, units[...], 0), axis=1, keepdims=True)
    patch = first + lax.broadcasted_iota(jnp.int32, (patch_count, 1), 0)
    query_ids = jnp.sum((patch >= ends_row).astype(jnp.int32), axis=1, keepdims=True)
    near = first - half + lax.broadcasted_iota(jnp.int32, (1, 2 * patch_count), 1)
    key_ids = jnp.sum((near >= ends_col).astype(jnp.int32), axis=0, keepdims=True)
    key_ids = jnp.where(near < 0, -1, key_ids)
    score_scale = 1.0 / math.sqrt(head_size)
    allowed = [
        query_ids[b * half : (b + 1) * half] == key_ids[:, b * half : (b + 3) * half]
        for b in range(2)
    ]
    sides = (low, high)
    contract = (((1,), (1,)), ((), ()))

    def one_head(head, carry):
        begin = pl.multiple_of(
            jnp.minimum((head * head_size) // LM_HEAD * LM_HEAD, width - window), LM_HEAD
        )
        columns = pl.ds(begin, window)
        lane = lax.broadcasted_iota(jnp.int32, (1, window), 1) + begin
        mine = (lane >= head * head_size) & (lane < (head + 1) * head_size)
        picked = jnp.where(mine, query[:, columns], 0)
        middle = lax.dot_general(
            picked, own[0, :, columns], contract, preferred_element_type=jnp.float32
        )
        for b in range(2):
            rows = slice(b * half, (b + 1) * half)
            edge = lax.dot_general(
                picked[rows], sides[b][0, :, columns], contract, preferred_element_type=jnp.float32
            )
            parts = [edge, middle[rows]] if b == 0 else [middle[rows], edge]
            scores = jnp.concatenate(parts, axis=1) * score_scale
            scores = jnp.where(allowed[b], scores, -1e30)
            shifted = jnp.exp(scores - jnp.max(scores, axis=1, keepdims=True))
            weights = (shifted / jnp.sum(shifted, axis=1, keepdims=True)).astype(jnp.bfloat16)
            split = half if b == 0 else 2 * half
            pieces = (low[1, :, columns], own[1, :, columns])
            if b == 1:
                pieces = (own[1, :, columns], high[1, :, columns])
            mixed = jnp.dot(
                weights[:, :split], pieces[0], preferred_element_type=jnp.float32
            ) + jnp.dot(weights[:, split:], pieces[1], preferred_element_type=jnp.float32)
            attended[rows, columns] = jnp.where(
                mine, mixed.astype(jnp.bfloat16), attended[rows, columns]
            )
        return carry

    lax.fori_loop(0, width // head_size, one_head, 0)


def normed_rows(values, gain):
    mean_square = jnp.mean(values * values, axis=1, keepdims=True)
    return (values * lax.rsqrt(mean_square + norm_epsilon) * gain).astype(jnp.bfloat16)


def norm_body(rows, gain, normed):
    normed[...] = normed_rows(rows[...].astype(jnp.float32), gain[...])


def places():
    me = lax.axis_index("tok")
    return me % 2, me // 2 % 2, me // 4


def hidden_body(first, second, *refs):
    pieces, (bias, residual, gain, normed, weight, hidden) = refs[:-6], refs[-6:]
    core, line, floor = places()
    rings = len(pieces) // 2
    for number, piece in enumerate(pieces):
        pair, depth, _ = piece.shape
        parity = core if number < rings else 1 - core
        level = lax.rem(floor - number % rings + rings, rings)
        for part in range(pair):
            head = level * 4 + (line ^ part) * 2 + parity
            weight[pl.ds(pl.multiple_of(head * depth, 16), depth), :] = piece[part]
    split = first.shape[1]
    total = jnp.dot(first[...], weight[:split], preferred_element_type=jnp.float32)
    total = total + jnp.dot(second[...], weight[split:], preferred_element_type=jnp.float32)
    total = total + bias[...] + residual[...].astype(jnp.float32)
    total = total.astype(jnp.bfloat16).astype(jnp.float32)
    tiles, units = hidden.shape[0], hidden.shape[1] // 4
    for tile in range(tiles):
        hidden[tile] = total[:, tile * LM_HEAD : (tile + 1) * LM_HEAD]
    merged = jnp.concatenate(
        [
            hidden[tile, pl.ds(part, units, stride=4), :]
            for part in range(4)
            for tile in range(tiles)
        ],
        axis=1,
    )
    normed[...] = normed_rows(merged, gain[...])


def pair_product(side, rows, pieces):
    if len(pieces) == 2:
        weight = jnp.concatenate([pieces[0][...], pieces[1][...]], axis=1)
        return jnp.dot(rows[...], weight, preferred_element_type=jnp.float32)
    depth = pieces[0].shape[0]
    total = None
    for number in range(2):
        begin = side if number == 0 else 1 - side
        columns = pl.ds(pl.multiple_of(begin * depth, LM_HEAD), depth)
        weight = jnp.concatenate(
            [pieces[2 * number][...], pieces[2 * number + 1][...]], axis=1
        )
        term = jnp.dot(rows[:, columns], weight, preferred_element_type=jnp.float32)
        total = term if total is None else total + term
    return total


def project_body(*refs, sizes, first):
    inputs = 4 + sum(sizes)
    sources, (bias, cosine, sine, place) = refs[:inputs], refs[inputs : inputs + 4]
    out_own, out_other, out_image = refs[inputs + 4 : inputs + 7]
    rows, held, arrived = refs[inputs + 7], refs[inputs + 8 : -1], refs[-1]
    targets, begin = [], 0
    for source in sources[:4]:
        targets.append(rows.at[begin : begin + source.shape[0]])
        begin += source.shape[0]
    copies = [
        pltpu.make_async_copy(source, target, arrived.at[number])
        for number, (source, target) in enumerate(zip(sources, targets + list(held)))
    ]
    for copy in copies:
        copy.start()
    side = lax.axis_index("groups")
    core, line, floor = places()
    rings = lax.axis_size("tok") // 4
    count = sources[0].shape[0]
    for copy in copies[:4]:
        copy.wait()
    begin = 0
    for number, size in enumerate(sizes):
        pieces = held[begin : begin + size]
        for piece in range(begin, begin + size):
            copies[4 + piece].wait()
        begin += size
        values = pair_product(side, rows, pieces)
        for part in range(2):
            block = lax.rem(floor - first - number + rings, rings) * 4
            block = block + (line ^ part) * 2 + core
            key = block < KV_HEADS
            lanes = pl.ds(pl.multiple_of(block * LM_HEAD, LM_HEAD), LM_HEAD)
            shifted = values[: 2 * count, part * LM_HEAD : (part + 1) * LM_HEAD] + bias[:, lanes]
            turning = jnp.where(key, cosine[...], 1.0)
            cross = jnp.where(key, sine[...], 0.0)
            turned = shifted * turning + pltpu.roll(shifted, LM_HEAD // 2, 1) * cross
            turned = turned.astype(jnp.bfloat16)
            out_own[2 * number + part] = turned[:count]
            out_other[2 * number + part] = turned[count:]
        placed = jnp.dot(
            place[...],
            values[2 * count :].astype(jnp.bfloat16),
            preferred_element_type=jnp.float32,
        )
        out_image[:, number * 2 * LM_HEAD : (number + 1) * 2 * LM_HEAD] = placed.astype(
            jnp.bfloat16
        )


def text_cache_body(*refs):
    pieces, out = refs[:-1], refs[-1]
    core, line, floor = places()
    rings = lax.axis_size("tok") // 4
    for parity, stacks in ((core, pieces[: len(pieces) // 2]), (1 - core, pieces[len(pieces) // 2 :])):
        number = 0
        for stack in stacks:
            for index in range(stack.shape[0]):
                block = lax.rem(floor - number // 2 + rings, rings) * 4
                block = block + (line ^ (number % 2)) * 2 + parity
                begin = pl.multiple_of(block * LM_HEAD, LM_HEAD)
                out[:, pl.ds(begin, LM_HEAD)] = stack[index]
                number += 1


def image_cache_body(*refs, orders):
    arrivals, (bias, cosine, sine, out) = refs[:-4], refs[-4:]
    device_count = arrivals[0].shape[0]
    depth = arrivals[0].shape[1]
    for source in range(device_count):
        rows = slice(source // 2 * depth, (source // 2 + 1) * depth)
        place = 0
        for arrival in arrivals:
            for part in range(arrival.shape[2] // LM_HEAD):
                block = orders[source][place]
                place += 1
                lanes = slice(block * LM_HEAD, (block + 1) * LM_HEAD)
                shifted = (
                    arrival[source, :, part * LM_HEAD : (part + 1) * LM_HEAD].astype(jnp.float32)
                    + bias[:, lanes]
                )
                if block < KV_HEADS:
                    shifted = (
                        shifted * cosine[rows]
                        + pltpu.roll(shifted, LM_HEAD // 2, 1) * sine[rows]
                    )
                out[rows, lanes] = shifted.astype(jnp.bfloat16)


def full_tables(positions):
    half_size = LM_HEAD // 2
    lane = jnp.arange(LM_HEAD, dtype=jnp.int32)
    index_pair = lane % half_size
    frequency = jnp.power(jnp.float32(rope_base), -2.0 * index_pair.astype(jnp.float32) / LM_HEAD)
    section = (index_pair >= half_size // 4).astype(jnp.int32) + (
        index_pair >= half_size // 4 + 3 * half_size // 8
    ).astype(jnp.int32)
    places = positions.astype(jnp.float32)
    chosen = jnp.zeros((positions.shape[1], LM_HEAD), jnp.float32)
    for axis_number in range(3):
        chosen = (
            chosen
            + places[axis_number][:, None] * (section == axis_number).astype(jnp.float32)[None, :]
        )
    angles = chosen * frequency[None, :]
    sign = jnp.where(lane < half_size, -1.0, 1.0)
    return jnp.cos(angles), jnp.sin(angles) * sign[None, :]


def per_device(*args):
    return permuted(*args)


def permuted(
    vis_query,
    vis_keyvalue,
    vis_residual,
    vis_out_weight,
    vis_out_bias,
    image_units,
    text_embed,
    lm_gain,
    lm_kv_weight,
    lm_kv_bias,
    text_positions,
    image_destination,
    image_positions,
):
    bf16, f32 = jnp.bfloat16, jnp.float32
    patch_count, vis_width = vis_query.shape
    head_size = vis_width // VIS_HEADS
    half_window = patch_count // 2
    count = lax.axis_size("tok")
    rings = count // 4
    side = lax.axis_index("groups")
    text_count, lm_width = text_embed.shape
    units = image_destination.shape[0]
    slot_count = image_positions.shape[1]
    capacity = slot_count // count

    def send(value, pairs, axis="tok"):
        return lax.ppermute(value, axis, pairs)

    sibling = [(i, i ^ 1) for i in range(count)]
    across = [(i, i ^ 2) for i in range(count)]
    upward = [(i, (i + 4) % count) for i in range(count)]
    peer = [(0, 1), (1, 0)]

    half_depth = lm_width // 2
    half = lax.dynamic_slice_in_dim(lm_kv_weight, side * half_depth, half_depth, 0)
    ring_halves = [half]
    for _ in range(1, rings):
        ring_halves.append(send(ring_halves[-1], upward))
    whole_across = send(lm_kv_weight, across)
    groups = [[lm_kv_weight, whole_across]]
    for step in range(1, rings):
        mine = [ring_halves[step], send(ring_halves[step], across)]
        peers = [send(mine[0], peer, "groups"), send(mine[1], peer, "groups")]
        groups.append(mine + peers)

    forward = [(i, i + 1) for i in range(count - 1)]
    backward = [(i + 1, i) for i in range(count - 1)]
    low = send(vis_keyvalue[:, patch_count - half_window :], forward)
    high = send(vis_keyvalue[:, :half_window], backward)

    rows_across = send(vis_out_weight, across)
    row_pair = jnp.stack([vis_out_weight, rows_across])
    row_mine = [row_pair]
    for _ in range(1, rings):
        row_mine.append(send(row_mine[-1], upward))
    row_other = [send(piece, sibling) for piece in row_mine]

    target = image_destination[:, 0]
    numbers = jnp.concatenate([text_positions, target])
    other_numbers = send(numbers, sibling)

    gain = lm_gain[None, :]
    normed_own = call_kernel(
        norm_body,
        jax.ShapeDtypeStruct((text_count, lm_width), bf16),
        text_embed,
        gain,
        cost=(text_count * lm_width * 8, 4 * text_count * lm_width),
    )
    normed_other = send(normed_own, sibling)

    attended = []
    wide = vis_width // 2
    for part in range(2):
        column = functools.partial(lambda part, i: (0, part), part)
        deep = functools.partial(lambda part, i: (0, 0, part), part)
        attended.append(
            call_kernel(
                functools.partial(attention_body, head_size=head_size, window=2 * LM_HEAD),
                jax.ShapeDtypeStruct((patch_count, wide), bf16),
                vis_query,
                vis_keyvalue,
                low,
                high,
                image_units[None, :],
                specs=[
                    pl.BlockSpec((patch_count, wide), column),
                    pl.BlockSpec((2, patch_count, wide), deep),
                    pl.BlockSpec((2, half_window, wide), deep),
                    pl.BlockSpec((2, half_window, wide), deep),
                    pl.BlockSpec(memory_space=pltpu.VMEM),
                ],
                cost=(patch_count * patch_count * vis_width * 12, 4 * patch_count * vis_width),
            )
        )

    depth = vis_out_weight.shape[0]
    core, _, _ = places()
    normed_image = call_kernel(
        hidden_body,
        jax.ShapeDtypeStruct((patch_count // 4, 4 * vis_width), bf16),
        *attended,
        *row_mine,
        *row_other,
        vis_out_bias[None, :],
        vis_residual,
        gain,
        scratch=[
            pltpu.VMEM((count * depth, vis_width), bf16),
            pltpu.VMEM((vis_width // LM_HEAD, patch_count, LM_HEAD), f32),
        ],
        cost=(2 * patch_count * vis_width * vis_width, 2 * vis_width * vis_width),
    )
    image_other = send(normed_image, sibling)

    other_target = other_numbers[text_count:]
    slot_own = target * (2 * capacity) + core * capacity + ranks_of(target)
    slot_other = other_target * (2 * capacity) + (1 - core) * capacity + ranks_of(other_target)
    slots = jnp.concatenate([slot_own, slot_other])
    place = (
        jnp.arange(2 * slot_count, dtype=jnp.int32)[:, None] == slots[None, :]
    ).astype(bf16)

    both_positions = jnp.concatenate([text_positions, other_numbers[:text_count]])
    cosine, sine = full_tables(jnp.broadcast_to(both_positions[None, :], (3, 2 * text_count)))
    bias = lm_kv_bias[None, :]

    blocks_own, blocks_other, arrivals = [], [], []
    for number, chosen in enumerate((groups[:-1], groups[-1:])):
        blocks = 2 * len(chosen)
        sources = [normed_own, normed_other, normed_image, image_other]
        sources += [piece for group in chosen for piece in group]
        whole = pl.BlockSpec(memory_space=pltpu.VMEM)
        kept, given, outgoing = call_kernel(
            functools.partial(
                project_body,
                sizes=[len(group) for group in chosen],
                first=0 if number == 0 else rings - 1,
            ),
            [jax.ShapeDtypeStruct((blocks, text_count, LM_HEAD), bf16)] * 2
            + [jax.ShapeDtypeStruct((2 * slot_count, blocks * LM_HEAD), bf16)],
            *sources,
            bias,
            cosine,
            sine,
            place,
            specs=[pl.BlockSpec(memory_space=pl.ANY)] * len(sources) + [whole] * 4,
            scratch=[pltpu.VMEM((2 * (text_count + units), lm_width), bf16)]
            + [pltpu.VMEM(source.shape, bf16) for source in sources[4:]]
            + [pltpu.SemaphoreType.DMA((len(sources),))],
            limit=24,
            cost=(
                4 * (text_count + units) * lm_width * LM_HEAD * blocks,
                4 * text_count * lm_width + 2 * lm_width * LM_HEAD * blocks,
            ),
        )
        blocks_own.append(kept)
        blocks_other.append(send(given, sibling))
        arrived = lax.all_to_all(outgoing, "tok", split_axis=0, concat_axis=0, tiled=True)
        arrivals.append(arrived.reshape(count, 2 * capacity, -1))

    text_cache = call_kernel(
        text_cache_body,
        jax.ShapeDtypeStruct((text_count, count * LM_HEAD), bf16),
        *blocks_own,
        *blocks_other,
    )
    orders = [
        [
            (source // 4 - step) % rings * 4 + (source // 2 % 2 ^ part) * 2 + source % 2
            for step in range(rings)
            for part in range(2)
        ]
        for source in range(count)
    ]
    image_cosine, image_sine = full_tables(image_positions)
    image_cache = call_kernel(
        functools.partial(image_cache_body, orders=orders),
        jax.ShapeDtypeStruct((slot_count, count * LM_HEAD), bf16),
        *arrivals,
        bias,
        image_cosine,
        image_sine,
    )
    return (text_cache, image_cache)


def fits(mesh, args):
    count = mesh.shape["tok"]
    weight = (args[8].shape[0], args[8].shape[1] // count)
    return (
        weight[1] == LM_HEAD
        and mesh.shape["groups"] == 2
        and count % 4 == 0
        and weight[0] % (2 * LM_HEAD) == 0
        and args[3].shape[0] // count % 16 == 0
        and args[12].shape[1] // (2 * count * count) % 8 == 0
    )


def solution(mesh):
    placed = (
        P(("groups", "tok"), None),
        P(None, ("groups", "tok"), None),
        P(("groups", "tok"), None),
        P("tok", None),
        P(),
        P("groups"),
        P(("groups", "tok"), None),
        P(),
        P(None, "tok"),
        P(),
        P(("groups", "tok")),
        P(("groups", "tok"), None),
        P(None, ("groups", "tok")),
    )

    specs = (P(("groups", "tok"), None), P(("groups", "tok"), None))

    def mapped(body):
        return jax.shard_map(
            body, mesh=mesh, in_specs=placed, out_specs=specs, check_vma=False
        )

    def chosen(*args):
        return mapped(per_device if fits(mesh, args) else per_device_gathered)(*args)

    return chosen
```

```python
import functools
import math

import jax
import jax.numpy as jnp
from jax import lax
from jax.experimental import pallas as pl
from jax.experimental.pallas import tpu as pltpu
from jax.sharding import PartitionSpec as P


VIS_HEADS = 16
KV_HEADS = 8
LM_HEAD = 128


norm_epsilon = 1e-06
rope_base = 1000000.0


def with_halo(block, sides, width):
    for axis, dim in sides:
        count = lax.axis_size(axis)
        forward = [(i, i + 1) for i in range(count - 1)]
        backward = [(target, source) for source, target in forward]
        low = lax.ppermute(
            lax.slice_in_dim(block, block.shape[dim] - width, None, axis=dim), axis, forward
        )
        high = lax.ppermute(lax.slice_in_dim(block, 0, width, axis=dim), axis, backward)
        block = jnp.concatenate([low, block, high], axis=dim)
    return block


def segment_ids(global_index, bounds):
    return jnp.sum((global_index[:, None] >= bounds[None, :]).astype(jnp.int32), axis=1) - 1


def rms_scale(rows, gain):
    values = rows.astype(jnp.float32)
    mean_square = jnp.mean(values * values, axis=1, keepdims=True)
    return (values * lax.rsqrt(mean_square + norm_epsilon) * gain).astype(jnp.bfloat16)


def rotation_tables(positions):
    half_size = LM_HEAD // 2
    index_pair = jnp.arange(half_size, dtype=jnp.int32)
    frequency = jnp.power(jnp.float32(rope_base), -2.0 * index_pair.astype(jnp.float32) / LM_HEAD)
    section = (index_pair >= half_size // 4).astype(jnp.int32) + (
        index_pair >= half_size // 4 + 3 * half_size // 8
    ).astype(jnp.int32)
    places = positions.astype(jnp.float32)
    chosen = jnp.zeros((positions.shape[1], half_size), jnp.float32)
    for axis_number in range(3):
        chosen = (
            chosen
            + places[axis_number][:, None] * (section == axis_number).astype(jnp.float32)[None, :]
        )
    angles = chosen * frequency[None, :]
    return jnp.cos(angles), jnp.sin(angles)


def rotate_keys(values, bias, positions):
    shifted = values + bias
    row_count = shifted.shape[0]
    kv_half = shifted.shape[1] // 2
    half_size = LM_HEAD // 2
    key_part = shifted[:, :kv_half].reshape(row_count, KV_HEADS, LM_HEAD)
    lower_half = key_part[:, :, :half_size]
    upper_half = key_part[:, :, half_size:]
    cosine, sine_part = rotation_tables(positions)
    cosine, sine_part = cosine[:, None, :], sine_part[:, None, :]
    turned = jnp.concatenate(
        [
            lower_half * cosine - upper_half * sine_part,
            upper_half * cosine + lower_half * sine_part,
        ],
        axis=2,
    )
    return jnp.concatenate(
        [turned.reshape(row_count, kv_half), shifted[:, kv_half:]], axis=1
    ).astype(jnp.bfloat16)


def head_attention(query_head, key_head, value_head, allowed, score_scale):
    scores = (
        jnp.einsum("qd,kd->qk", query_head, key_head, preferred_element_type=jnp.float32)
        * score_scale
    )
    scores = jnp.where(allowed, scores, -1e30)
    row_max = jnp.max(scores, axis=1, keepdims=True)
    shifted = jnp.exp(scores - row_max)
    weights = (shifted / jnp.sum(shifted, axis=1, keepdims=True)).astype(jnp.bfloat16)
    return jnp.dot(weights, value_head, preferred_element_type=jnp.float32).astype(jnp.bfloat16)


def project_rows(normed, kv_weight):
    return jnp.dot(
        normed,
        lax.all_gather(kv_weight, "tok", axis=1, tiled=True),
        preferred_element_type=jnp.float32,
    )


def ranks_of(target):
    unit_count = target.shape[0]
    same_target = target[:, None] == target[None, :]
    earlier = (
        jnp.arange(unit_count, dtype=jnp.int32)[None, :]
        < jnp.arange(unit_count, dtype=jnp.int32)[:, None]
    )
    return jnp.sum((same_target & earlier).astype(jnp.int32), axis=1)


def per_device_gathered(
    vis_query,
    vis_keyvalue,
    vis_residual,
    vis_out_weight,
    vis_out_bias,
    image_units,
    text_embed,
    lm_gain,
    lm_kv_weight,
    lm_kv_bias,
    text_positions,
    image_destination,
    image_positions,
):
    patch_count, vis_width = vis_query.shape
    head_size = vis_width // VIS_HEADS
    half_window = patch_count // 2
    device_count = lax.axis_size("tok")
    device_index = lax.axis_index("tok")
    nearby = with_halo(vis_keyvalue, (("tok", 1),), half_window)
    bounds = jnp.concatenate([jnp.zeros((1,), jnp.int32), jnp.cumsum(4 * image_units)])
    offset = device_index * patch_count
    query_ids = segment_ids(offset + jnp.arange(patch_count, dtype=jnp.int32), bounds)
    key_ids = segment_ids(
        offset - half_window + jnp.arange(2 * patch_count, dtype=jnp.int32), bounds
    )
    allowed = query_ids[:, None] == key_ids[None, :]
    score_scale = 1.0 / math.sqrt(head_size)
    query_heads = vis_query.reshape(patch_count, VIS_HEADS, head_size).transpose(1, 0, 2)
    key_heads = nearby[0].reshape(2 * patch_count, VIS_HEADS, head_size).transpose(1, 0, 2)
    value_heads = nearby[1].reshape(2 * patch_count, VIS_HEADS, head_size).transpose(1, 0, 2)
    attended = lax.map(
        lambda pieces: head_attention(pieces[0], pieces[1], pieces[2], allowed, score_scale),
        (query_heads, key_heads, value_heads),
    )
    attended = attended.transpose(1, 0, 2).reshape(patch_count, vis_width)
    projected = jnp.dot(
        attended,
        lax.all_gather(vis_out_weight, "tok", axis=0, tiled=True),
        preferred_element_type=jnp.float32,
    )
    vis_hidden = (projected + vis_out_bias + vis_residual.astype(jnp.float32)).astype(jnp.bfloat16)
    merged = vis_hidden.reshape(patch_count // 4, 4 * vis_width)
    target = image_destination[:, 0]
    slot_count = image_positions.shape[1]
    capacity = slot_count // device_count
    slot_index = target * capacity + ranks_of(target)
    text_count = text_embed.shape[0]
    kv_width = lm_kv_bias.shape[0]
    normed = rms_scale(jnp.concatenate([text_embed, merged], axis=0), lm_gain)
    projected_rows = project_rows(normed, lm_kv_weight)
    text_values = projected_rows[:text_count]
    outgoing = (
        jnp.zeros((slot_count, kv_width), jnp.float32)
        .at[slot_index]
        .set(projected_rows[text_count:])
    )
    image_values = lax.all_to_all(outgoing, "tok", split_axis=0, concat_axis=0, tiled=True)
    text_cache = rotate_keys(
        text_values, lm_kv_bias, jnp.broadcast_to(text_positions[None, :], (3, text_count))
    )
    image_cache = rotate_keys(image_values, lm_kv_bias, image_positions)
    return (text_cache, image_cache)


def call_kernel(body, outs, *args, specs=None, scratch=(), cost=None, limit=10):
    flops, moved = cost if cost else (0, 0)
    return pl.pallas_call(
        body,
        out_shape=outs,
        grid=(1,) if specs else (),
        in_specs=specs or [pl.BlockSpec(memory_space=pltpu.VMEM)] * len(args),
        out_specs=jax.tree.map(lambda _: pl.BlockSpec(memory_space=pltpu.VMEM), outs),
        scratch_shapes=list(scratch),
        cost_estimate=pl.CostEstimate(flops=flops, bytes_accessed=moved, transcendentals=0),
        compiler_params=pltpu.CompilerParams(vmem_limit_bytes=limit << 20),
    )(*args)


def attention_body(query, own, low, high, units, attended, *, head_size, window):
    patch_count, width = query.shape
    half = patch_count // 2
    count = units.shape[1]
    first = lax.axis_index("tok") * patch_count
    wide = lax.broadcasted_iota(jnp.int32, (count, count), 0)
    across = lax.broadcasted_iota(jnp.int32, (count, count), 1)
    units_col = jnp.sum(jnp.where(wide == across, units[...], 0), axis=1, keepdims=True)
    ends_row = 4 * jnp.sum(jnp.where(wide <= across, units_col, 0), axis=0, keepdims=True)
    ends_col = 4 * jnp.sum(jnp.where(across <= wide, units[...], 0), axis=1, keepdims=True)
    patch = first + lax.broadcasted_iota(jnp.int32, (patch_count, 1), 0)
    query_ids = jnp.sum((patch >= ends_row).astype(jnp.int32), axis=1, keepdims=True)
    near = first - half + lax.broadcasted_iota(jnp.int32, (1, 2 * patch_count), 1)
    key_ids = jnp.sum((near >= ends_col).astype(jnp.int32), axis=0, keepdims=True)
    key_ids = jnp.where(near < 0, -1, key_ids)
    score_scale = 1.0 / math.sqrt(head_size)
    allowed = [
        query_ids[b * half : (b + 1) * half] == key_ids[:, b * half : (b + 3) * half]
        for b in range(2)
    ]
    sides = (low, high)
    contract = (((1,), (1,)), ((), ()))

    def one_head(head, carry):
        begin = pl.multiple_of(
            jnp.minimum((head * head_size) // LM_HEAD * LM_HEAD, width - window), LM_HEAD
        )
        columns = pl.ds(begin, window)
        lane = lax.broadcasted_iota(jnp.int32, (1, window), 1) + begin
        mine = (lane >= head * head_size) & (lane < (head + 1) * head_size)
        picked = jnp.where(mine, query[:, columns], 0)
        middle = lax.dot_general(
            picked, own[0, :, columns], contract, preferred_element_type=jnp.float32
        )
        for b in range(2):
            rows = slice(b * half, (b + 1) * half)
            edge = lax.dot_general(
                picked[rows], sides[b][0, :, columns], contract, preferred_element_type=jnp.float32
            )
            parts = [edge, middle[rows]] if b == 0 else [middle[rows], edge]
            scores = jnp.concatenate(parts, axis=1) * score_scale
            scores = jnp.where(allowed[b], scores, -1e30)
            shifted = jnp.exp(scores - jnp.max(scores, axis=1, keepdims=True))
            weights = (shifted / jnp.sum(shifted, axis=1, keepdims=True)).astype(jnp.bfloat16)
            split = half if b == 0 else 2 * half
            pieces = (low[1, :, columns], own[1, :, columns])
            if b == 1:
                pieces = (own[1, :, columns], high[1, :, columns])
            mixed = jnp.dot(
                weights[:, :split], pieces[0], preferred_element_type=jnp.float32
            ) + jnp.dot(weights[:, split:], pieces[1], preferred_element_type=jnp.float32)
            attended[rows, columns] = jnp.where(
                mine, mixed.astype(jnp.bfloat16), attended[rows, columns]
            )
        return carry

    lax.fori_loop(0, width // head_size, one_head, 0)


def normed_rows(values, gain):
    mean_square = jnp.mean(values * values, axis=1, keepdims=True)
    return (values * lax.rsqrt(mean_square + norm_epsilon) * gain).astype(jnp.bfloat16)


def norm_body(rows, gain, normed):
    normed[...] = normed_rows(rows[...].astype(jnp.float32), gain[...])


def places():
    me = lax.axis_index("tok")
    return me % 2, me // 2 % 2, me // 4


def hidden_body(first, second, *refs):
    pieces, (bias, residual, gain, normed, weight, hidden) = refs[:-6], refs[-6:]
    core, line, floor = places()
    rings = len(pieces) // 2
    for number, piece in enumerate(pieces):
        pair, depth, _ = piece.shape
        parity = core if number < rings else 1 - core
        level = lax.rem(floor - number % rings + rings, rings)
        for part in range(pair):
            head = level * 4 + (line ^ part) * 2 + parity
            weight[pl.ds(pl.multiple_of(head * depth, 16), depth), :] = piece[part]
    split = first.shape[1]
    total = jnp.dot(first[...], weight[:split], preferred_element_type=jnp.float32)
    total = total + jnp.dot(second[...], weight[split:], preferred_element_type=jnp.float32)
    total = total + bias[...] + residual[...].astype(jnp.float32)
    total = total.astype(jnp.bfloat16).astype(jnp.float32)
    tiles, units = hidden.shape[0], hidden.shape[1] // 4
    for tile in range(tiles):
        hidden[tile] = total[:, tile * LM_HEAD : (tile + 1) * LM_HEAD]
    merged = jnp.concatenate(
        [
            hidden[tile, pl.ds(part, units, stride=4), :]
            for part in range(4)
            for tile in range(tiles)
        ],
        axis=1,
    )
    normed[...] = normed_rows(merged, gain[...])


def pair_product(side, rows, pieces):
    if len(pieces) == 2:
        weight = jnp.concatenate([pieces[0][...], pieces[1][...]], axis=1)
        return jnp.dot(rows[...], weight, preferred_element_type=jnp.float32)
    depth = pieces[0].shape[0]
    total = None
    for number in range(2):
        begin = side if number == 0 else 1 - side
        columns = pl.ds(pl.multiple_of(begin * depth, LM_HEAD), depth)
        weight = jnp.concatenate(
            [pieces[2 * number][...], pieces[2 * number + 1][...]], axis=1
        )
        term = jnp.dot(rows[:, columns], weight, preferred_element_type=jnp.float32)
        total = term if total is None else total + term
    return total


def project_body(*refs, levels, sizes, fresh, carried):
    core, line, floor = places()
    side = lax.axis_index("groups")
    rings = lax.axis_size("tok") // 4
    refs = list(refs)
    sources = [refs.pop(0) for _ in range(4 if fresh else 1)]
    pieces = [refs.pop(0) for _ in range(sum(sizes))]
    earlier = refs.pop(0) if carried else None
    bias, cosine, sine, place, out_own, out_other, out_image = [refs.pop(0) for _ in range(7)]
    copies = []
    if fresh:
        rows, held, arrived = refs[0], refs[1:-1], refs[-1]
        targets, begin = [], 0
        for source in sources:
            targets.append(rows.at[begin : begin + source.shape[0]])
            begin += source.shape[0]
        copies = [
            pltpu.make_async_copy(source, target, arrived.at[number])
            for number, (source, target) in enumerate(
                zip(sources + pieces, targets + list(held))
            )
        ]
        for copy in copies:
            copy.start()
        for copy in copies[:4]:
            copy.wait()
        pieces = held
    else:
        rows = sources[0]
    shift = 0
    if carried:
        shift = earlier.shape[1]
        out_image[:, :shift] = earlier[...]
    count = out_own.shape[1]
    begin = 0
    for number, size in enumerate(sizes):
        mine = pieces[begin : begin + size]
        if fresh:
            for piece in range(begin, begin + size):
                copies[4 + piece].wait()
        begin += size
        values = pair_product(side, rows, mine)
        for part in range(2):
            block = lax.rem(floor - levels[number] + rings, rings) * 4
            block = block + (line ^ part) * 2 + core
            key = block < KV_HEADS
            lanes = pl.ds(pl.multiple_of(block * LM_HEAD, LM_HEAD), LM_HEAD)
            shifted = values[: 2 * count, part * LM_HEAD : (part + 1) * LM_HEAD] + bias[:, lanes]
            turning = jnp.where(key, cosine[...], 1.0)
            cross = jnp.where(key, sine[...], 0.0)
            turned = shifted * turning + pltpu.roll(shifted, LM_HEAD // 2, 1) * cross
            turned = turned.astype(jnp.bfloat16)
            out_own[2 * number + part] = turned[:count]
            out_other[2 * number + part] = turned[count:]
        placed = jnp.dot(
            place[...],
            values[2 * count :].astype(jnp.bfloat16),
            preferred_element_type=jnp.float32,
        )
        lanes = slice(shift + number * 2 * LM_HEAD, shift + (number + 1) * 2 * LM_HEAD)
        out_image[:, lanes] = placed.astype(jnp.bfloat16)


def text_cache_body(*refs, levels):
    pieces, out = refs[:-1], refs[-1]
    core, line, floor = places()
    rings = lax.axis_size("tok") // 4
    half = len(pieces) // 2
    for parity, stacks in ((core, pieces[:half]), (1 - core, pieces[half:])):
        number = 0
        for stack in stacks:
            for index in range(stack.shape[0]):
                block = lax.rem(floor - levels[number // 2] + rings, rings) * 4
                block = block + (line ^ (number % 2)) * 2 + parity
                begin = pl.multiple_of(block * LM_HEAD, LM_HEAD)
                out[:, pl.ds(begin, LM_HEAD)] = stack[index]
                number += 1


def image_cache_body(*refs, orders):
    arrivals, (bias, cosine, sine, out) = refs[:-4], refs[-4:]
    device_count = arrivals[0].shape[0]
    depth = arrivals[0].shape[1]
    for source in range(device_count):
        rows = slice(source // 2 * depth, (source // 2 + 1) * depth)
        place = 0
        for arrival in arrivals:
            for part in range(arrival.shape[2] // LM_HEAD):
                block = orders[source][place]
                place += 1
                lanes = slice(block * LM_HEAD, (block + 1) * LM_HEAD)
                shifted = (
                    arrival[source, :, part * LM_HEAD : (part + 1) * LM_HEAD].astype(jnp.float32)
                    + bias[:, lanes]
                )
                if block < KV_HEADS:
                    shifted = (
                        shifted * cosine[rows]
                        + pltpu.roll(shifted, LM_HEAD // 2, 1) * sine[rows]
                    )
                out[rows, lanes] = shifted.astype(jnp.bfloat16)


def full_tables(positions):
    half_size = LM_HEAD // 2
    lane = jnp.arange(LM_HEAD, dtype=jnp.int32)
    index_pair = lane % half_size
    frequency = jnp.power(jnp.float32(rope_base), -2.0 * index_pair.astype(jnp.float32) / LM_HEAD)
    section = (index_pair >= half_size // 4).astype(jnp.int32) + (
        index_pair >= half_size // 4 + 3 * half_size // 8
    ).astype(jnp.int32)
    places = positions.astype(jnp.float32)
    chosen = jnp.zeros((positions.shape[1], LM_HEAD), jnp.float32)
    for axis_number in range(3):
        chosen = (
            chosen
            + places[axis_number][:, None] * (section == axis_number).astype(jnp.float32)[None, :]
        )
    angles = chosen * frequency[None, :]
    sign = jnp.where(lane < half_size, -1.0, 1.0)
    return jnp.cos(angles), jnp.sin(angles) * sign[None, :]


def per_device(*args):
    return permuted(*args)


def permuted(
    vis_query,
    vis_keyvalue,
    vis_residual,
    vis_out_weight,
    vis_out_bias,
    image_units,
    text_embed,
    lm_gain,
    lm_kv_weight,
    lm_kv_bias,
    text_positions,
    image_destination,
    image_positions,
):
    bf16, f32 = jnp.bfloat16, jnp.float32
    patch_count, vis_width = vis_query.shape
    head_size = vis_width // VIS_HEADS
    half_window = patch_count // 2
    count = lax.axis_size("tok")
    rings = count // 4
    side = lax.axis_index("groups")
    text_count, lm_width = text_embed.shape
    units = image_destination.shape[0]
    slot_count = image_positions.shape[1]
    capacity = slot_count // count

    def send(value, pairs, axis="tok"):
        return lax.ppermute(value, axis, pairs)

    sibling = [(i, i ^ 1) for i in range(count)]
    across = [(i, i ^ 2) for i in range(count)]
    upward = [(i, (i + 4) % count) for i in range(count)]
    peer = [(0, 1), (1, 0)]

    half_depth = lm_width // 2
    half = lax.dynamic_slice_in_dim(lm_kv_weight, side * half_depth, half_depth, 0)
    ring_halves = [half]
    for _ in range(1, rings):
        ring_halves.append(send(ring_halves[-1], upward))
    whole_across = send(lm_kv_weight, across)
    groups = [[lm_kv_weight, whole_across]]
    for step in range(1, rings):
        mine = [ring_halves[step], send(ring_halves[step], across)]
        peers = [send(mine[0], peer, "groups"), send(mine[1], peer, "groups")]
        groups.append(mine + peers)

    forward = [(i, i + 1) for i in range(count - 1)]
    backward = [(i + 1, i) for i in range(count - 1)]
    low = send(vis_keyvalue[:, patch_count - half_window :], forward)
    high = send(vis_keyvalue[:, :half_window], backward)

    rows_across = send(vis_out_weight, across)
    row_pair = jnp.stack([vis_out_weight, rows_across])
    row_mine = [row_pair]
    for _ in range(1, rings):
        row_mine.append(send(row_mine[-1], upward))
    row_other = [send(piece, sibling) for piece in row_mine]

    target = image_destination[:, 0]
    numbers = jnp.concatenate([text_positions, target])
    other_numbers = send(numbers, sibling)

    gain = lm_gain[None, :]
    normed_own = call_kernel(
        norm_body,
        jax.ShapeDtypeStruct((text_count, lm_width), bf16),
        text_embed,
        gain,
        cost=(text_count * lm_width * 8, 4 * text_count * lm_width),
    )
    normed_other = send(normed_own, sibling)

    attended = []
    wide = vis_width // 2
    for part in range(2):
        column = functools.partial(lambda part, i: (0, part), part)
        deep = functools.partial(lambda part, i: (0, 0, part), part)
        attended.append(
            call_kernel(
                functools.partial(attention_body, head_size=head_size, window=2 * LM_HEAD),
                jax.ShapeDtypeStruct((patch_count, wide), bf16),
                vis_query,
                vis_keyvalue,
                low,
                high,
                image_units[None, :],
                specs=[
                    pl.BlockSpec((patch_count, wide), column),
                    pl.BlockSpec((2, patch_count, wide), deep),
                    pl.BlockSpec((2, half_window, wide), deep),
                    pl.BlockSpec((2, half_window, wide), deep),
                    pl.BlockSpec(memory_space=pltpu.VMEM),
                ],
                cost=(patch_count * patch_count * vis_width * 12, 4 * patch_count * vis_width),
            )
        )

    depth = vis_out_weight.shape[0]
    core, _, _ = places()
    normed_image = call_kernel(
        hidden_body,
        jax.ShapeDtypeStruct((patch_count // 4, 4 * vis_width), bf16),
        *attended,
        *row_mine,
        *row_other,
        vis_out_bias[None, :],
        vis_residual,
        gain,
        scratch=[
            pltpu.VMEM((count * depth, vis_width), bf16),
            pltpu.VMEM((vis_width // LM_HEAD, patch_count, LM_HEAD), f32),
        ],
        cost=(2 * patch_count * vis_width * vis_width, 2 * vis_width * vis_width),
    )
    image_other = send(normed_image, sibling)

    other_target = other_numbers[text_count:]
    slot_own = target * (2 * capacity) + core * capacity + ranks_of(target)
    slot_other = other_target * (2 * capacity) + (1 - core) * capacity + ranks_of(other_target)
    slots = jnp.concatenate([slot_own, slot_other])
    place = (
        jnp.arange(2 * slot_count, dtype=jnp.int32)[:, None] == slots[None, :]
    ).astype(bf16)

    both_positions = jnp.concatenate([text_positions, other_numbers[:text_count]])
    cosine, sine = full_tables(jnp.broadcast_to(both_positions[None, :], (3, 2 * text_count)))
    bias = lm_kv_bias[None, :]

    blocks_own, blocks_other, arrivals = [], [], []
    calls = [list(range(1, rings - 1)), [0], [rings - 1]]
    row_sources = [normed_own, normed_other, normed_image, image_other]
    row_total = 2 * (text_count + units)
    rows, outgoing = None, None
    for number, levels in enumerate(calls):
        blocks = 2 * len(levels)
        fresh, carried = number == 0, number == 1
        pieces = [piece for level in levels for piece in groups[level]]
        width = blocks * LM_HEAD + (outgoing.shape[1] if carried else 0)
        whole = pl.BlockSpec(memory_space=pltpu.VMEM)
        outs = [jax.ShapeDtypeStruct((blocks, text_count, LM_HEAD), bf16)] * 2
        outs += [jax.ShapeDtypeStruct((2 * slot_count, width), bf16)]
        inputs = [rows] + pieces + ([outgoing] if carried else [])
        specs, scratch = None, ()
        if fresh:
            outs += [jax.ShapeDtypeStruct((row_total, lm_width), bf16)]
            inputs = row_sources + pieces
            specs = [pl.BlockSpec(memory_space=pl.ANY)] * len(inputs) + [whole] * 4
            scratch = [pltpu.VMEM(piece.shape, bf16) for piece in pieces]
            scratch += [pltpu.SemaphoreType.DMA((len(inputs),))]
        results = call_kernel(
            functools.partial(
                project_body,
                levels=levels,
                sizes=[len(groups[level]) for level in levels],
                fresh=fresh,
                carried=carried,
            ),
            outs,
            *inputs,
            bias,
            cosine,
            sine,
            place,
            specs=specs,
            scratch=scratch,
            limit=24 if fresh else 16,
            cost=(
                2 * row_total * lm_width * LM_HEAD * blocks,
                2 * row_total * lm_width + 2 * lm_width * LM_HEAD * blocks,
            ),
        )
        kept, given, outgoing = results[:3]
        rows = results[3] if fresh else rows
        blocks_own.append(kept)
        blocks_other.append(send(given, sibling))
        if number == 0:
            continue
        arrived = lax.all_to_all(outgoing, "tok", split_axis=0, concat_axis=0, tiled=True)
        arrivals.append(arrived.reshape(count, 2 * capacity, -1))

    levels = sum(calls, [])
    text_cache = call_kernel(
        functools.partial(text_cache_body, levels=levels),
        jax.ShapeDtypeStruct((text_count, count * LM_HEAD), bf16),
        *blocks_own,
        *blocks_other,
    )
    orders = [
        [
            (source // 4 - level) % rings * 4 + (source // 2 % 2 ^ part) * 2 + source % 2
            for level in levels
            for part in range(2)
        ]
        for source in range(count)
    ]
    image_cosine, image_sine = full_tables(image_positions)
    image_cache = call_kernel(
        functools.partial(image_cache_body, orders=orders),
        jax.ShapeDtypeStruct((slot_count, count * LM_HEAD), bf16),
        *arrivals,
        bias,
        image_cosine,
        image_sine,
    )
    return (text_cache, image_cache)


def fits(mesh, args):
    count = mesh.shape["tok"]
    weight = (args[8].shape[0], args[8].shape[1] // count)
    return (
        weight[1] == LM_HEAD
        and mesh.shape["groups"] == 2
        and count % 4 == 0
        and weight[0] % (2 * LM_HEAD) == 0
        and args[3].shape[0] // count % 16 == 0
        and args[12].shape[1] // (2 * count * count) % 8 == 0
    )


def solution(mesh):
    placed = (
        P(("groups", "tok"), None),
        P(None, ("groups", "tok"), None),
        P(("groups", "tok"), None),
        P("tok", None),
        P(),
        P("groups"),
        P(("groups", "tok"), None),
        P(),
        P(None, "tok"),
        P(),
        P(("groups", "tok")),
        P(("groups", "tok"), None),
        P(None, ("groups", "tok")),
    )

    specs = (P(("groups", "tok"), None), P(("groups", "tok"), None))

    def mapped(body):
        return jax.shard_map(
            body, mesh=mesh, in_specs=placed, out_specs=specs, check_vma=False
        )

    def chosen(*args):
        return mapped(per_device if fits(mesh, args) else per_device_gathered)(*args)

    return chosen
```
